256 devices in a mesh: dp: 16 (over z, core), mp: 16 (over x, y).
Axes of the slice: x: 4, y: 4, z: 8, core: 2. Of those that a mesh axis runs over, the one named last changes fastest.
Arguments:
- grad_parts: bfloat16 [16, 512, 256, 256], P('dp', 'mp'), may hold values from -0.25 to 0.25
- left_stats: float32 [16, 16, 4, 256, 256], P('dp', 'mp'), may hold values from -6 to 6
- right_stats: float32 [16, 16, 4, 256, 256], P('dp', 'mp'), may hold values from -6 to 6
- left_root: bfloat16 [16, 16, 4, 256, 256], P('dp', 'mp'), may hold values from -4 to 4
- right_root: bfloat16 [16, 16, 4, 256, 256], P('dp', 'mp'), may hold values from -4 to 4
- owners: int32 [512], replicated, may hold values from 0 to 15, as said below
Outputs:
- direction: bfloat16 [512, 256, 256], P('mp')
- left_updated: float32 [16, 16, 4, 256, 256], P('dp', 'mp')
- right_updated: float32 [16, 16, 4, 256, 256], P('dp', 'mp')
The draws below stay inside these ranges and needn't reach their ends.
Inputs may be any that keep to these rules, and one draw needn't show every extreme that they name: The blocks b with the same b // 2 have distinct owners. Among the blocks of one row, no owner is named more than 4 times, and in every row some owner is named exactly 4 times.
All inputs are finite; a program needn't handle non-finite values.
Results may differ from the reference program's by a relative error of at most 0.02.
Values may be sent and summed in bfloat16 or wider, within the bound.
No kernel may reach another device: no remote copies, remote signals or barrier semaphores. Data moves between devices by JAX's collectives and lax.ppermute only.
A program may use at most 64 MiB of HBM per device.

```python
import jax
import jax.numpy as jnp
from jax import lax

B = 256
BD = 2
SLOTS = 4
REPLICAS = 16
OWNERS = 16
NB = 512


def draw_owners(key, part):

    def one_row(row_key):
        key_sigma, key_rank = jax.random.split(row_key, 2)
        sigma = jax.random.permutation(key_sigma, OWNERS).astype(jnp.int32)
        ranks = jax.random.permutation(key_rank, OWNERS).astype(jnp.int32)
        columns = jnp.arange(BD, dtype=jnp.int32)
        classes = ((ranks[:, None] + columns[None, :]) % (OWNERS - 1)).astype(jnp.int32)
        chosen = sigma[1 + classes]
        heavy_holder = (ranks[:, None] < SLOTS) & (columns[None, :] == 0)
        chosen = jnp.where(heavy_holder, sigma[0], chosen)
        return chosen.astype(jnp.int32)
    row_keys = jax.random.split(jax.random.fold_in(key, 7), REPLICAS)
    table = jax.vmap(one_row)(row_keys)
    return jnp.transpose(table, (1, 0, 2)).reshape(NB).astype(jnp.int32)


def block_scale(stream_key, dims, cuts, least, high):
    loudness, own = 1.0, jax.random.fold_in(stream_key, 6)
    for position, parts in cuts:
        heights = jnp.exp(jax.random.uniform(jax.random.fold_in(own, position), (parts,), jnp.float32, least / len(cuts), high / len(cuts)))
        loudness = loudness * jnp.repeat(heights, dims[position] // parts).reshape([-1 if axis == position else 1 for axis in range(len(dims))])
    return loudness


def bell_draw(rng, shape, spread, limit, cuts=(), kind=jnp.bfloat16):
    values = spread * jax.random.normal(rng, shape, jnp.float32)
    if cuts:
        values = values * block_scale(rng, shape, cuts, -0.22, 0.18)
    return jnp.clip(values, -limit, limit).astype(kind)


def setup_inputs(seed: int = 0) -> dict:
    keys = jax.random.split(jax.random.key(seed), 7)
    grad_parts = bell_draw(keys[0], (REPLICAS, NB, B, B), (0.25 / B ** 0.5), 0.25, ((0, 16), (1, 16)))
    left_stats = bell_draw(keys[1], (REPLICAS, OWNERS, SLOTS, B, B), 1.0, 6.0, ((0, 16), (1, 16)), jnp.float32)
    right_stats = bell_draw(keys[2], (REPLICAS, OWNERS, SLOTS, B, B), 1.0, 6.0, ((0, 16), (1, 16)), jnp.float32)
    left_root = bell_draw(keys[3], (REPLICAS, OWNERS, SLOTS, B, B), (B ** -0.25), 4.0, ((0, 16), (1, 16)))
    right_root = bell_draw(keys[4], (REPLICAS, OWNERS, SLOTS, B, B), (B ** -0.25), 4.0, ((0, 16), (1, 16)))
    owners = draw_owners(jax.random.fold_in(keys[6], 71), 0)
    return dict(grad_parts=grad_parts, left_stats=left_stats, right_stats=right_stats, left_root=left_root, right_root=right_root, owners=owners)


def reference(grad_parts, left_stats, right_stats, left_root, right_root, owners):
    def add_part(index, running):
        return running + lax.dynamic_index_in_dim(grad_parts, index, 0, keepdims=False).astype(jnp.float32)

    summed = lax.fori_loop(0, REPLICAS, add_part, jnp.zeros(grad_parts.shape[1:], jnp.float32))
    grad_blocks = summed.astype(jnp.bfloat16)
    block_ids = jnp.arange(NB, dtype=jnp.int32)
    row_of = (block_ids % (BD * REPLICAS)) // BD
    earlier = (row_of[:, None] == row_of[None, :]) & (owners[:, None] == owners[None, :]) & (block_ids[None, :] < block_ids[:, None])
    slot_of = jnp.sum(earlier.astype(jnp.int32), axis=1).astype(jnp.int32)
    slot_key = ((row_of * OWNERS + owners) * SLOTS + slot_of).astype(jnp.int32)
    slot_total = REPLICAS * OWNERS * SLOTS
    source_ids = jnp.zeros((slot_total,), jnp.int32).at[slot_key].set(block_ids)
    filled = jnp.zeros((slot_total,), jnp.int32).at[slot_key].set(jnp.ones((NB,), jnp.int32))
    picked = jnp.take(grad_blocks, source_ids, axis=0)
    owned_grad = jnp.where(filled[:, None, None] > 0, picked, jnp.zeros_like(picked)).astype(jnp.bfloat16)
    left_flat = left_stats.reshape(slot_total, B, B)
    right_flat = right_stats.reshape(slot_total, B, B)
    lroot_flat = left_root.reshape(slot_total, B, B)
    rroot_flat = right_root.reshape(slot_total, B, B)

    def one_slot(items):
        grad_one, left_one, right_one, lroot_one, rroot_one = items
        grad_wide = grad_one.astype(jnp.float32)
        left_next = left_one + jnp.dot(grad_wide, grad_wide.T)
        right_next = right_one + jnp.dot(grad_wide.T, grad_wide)
        half_step = jnp.dot(lroot_one.astype(jnp.float32), grad_wide).astype(jnp.bfloat16)
        result = jnp.dot(half_step.astype(jnp.float32), rroot_one.astype(jnp.float32)).astype(jnp.bfloat16)
        return left_next, right_next, result

    left_next, right_next, precond = lax.map(one_slot, (owned_grad, left_flat, right_flat, lroot_flat, rroot_flat))
    direction = jnp.take(precond, slot_key, axis=0)
    return direction, left_next.reshape(left_stats.shape), right_next.reshape(right_stats.shape)
```

```python
import jax
import jax.numpy as jnp
from jax import lax
from jax.experimental import pallas as pl
from jax.experimental.pallas import tpu as pltpu
from jax.sharding import Mesh
from jax.sharding import PartitionSpec as P

DP = ("z", "core")
F32 = jnp.float32
BF16 = jnp.bfloat16


def pick_kernel(src_ref, val_ref, out_ref):
    def one(i, carry):
        src = src_ref[i]
        piece = val_ref[jnp.maximum(src, 0)]
        out_ref[i] = jnp.where(src >= 0, piece, jnp.zeros_like(piece))
        return carry

    lax.fori_loop(0, out_ref.shape[0], one, 0, unroll=8)


def pick(src, values, count):
    return pl.pallas_call(
        pick_kernel,
        out_shape=jax.ShapeDtypeStruct((count, *values.shape[1:]), values.dtype),
        in_specs=[
            pl.BlockSpec(memory_space=pltpu.SMEM),
            pl.BlockSpec(memory_space=pltpu.VMEM),
        ],
        out_specs=pl.BlockSpec(memory_space=pltpu.VMEM),
        name="pick",
    )(src, values)


def precond_kernel(own_ref, left_ref, right_ref, out_ref):
    peers, _, rows, cols = own_ref.shape
    for s in range(own_ref.shape[1]):
        own = own_ref[:, s].reshape(peers * rows, cols)
        half = jnp.dot(left_ref[s], own, preferred_element_type=F32).astype(BF16)
        full = jnp.dot(half, right_ref[s], preferred_element_type=F32).astype(BF16)
        out_ref[:, s] = full.reshape(peers, rows, cols)


def precondition(own, left_root, right_root):
    vmem = pl.BlockSpec(memory_space=pltpu.VMEM)
    return pl.pallas_call(
        precond_kernel,
        out_shape=jax.ShapeDtypeStruct(own.shape, BF16),
        in_specs=[vmem, vmem, vmem],
        out_specs=vmem,
        name="precond",
    )(own, left_root, right_root)


def per_device(grad_parts, left_stats, right_stats, left_root, right_root, owners):
    zs = lax.axis_size("z")
    mp = lax.axis_size("mp")
    z = lax.axis_index("z")
    core = lax.axis_index("core")
    dp = z * 2 + core
    _, per_shard, rows, cols = grad_parts.shape
    held = per_shard // (2 * zs)
    slots = left_stats.shape[2]
    piece = rows // mp
    up = [(i, (i + 1) % zs) for i in range(zs)]
    down = [(i, (i - 1) % zs) for i in range(zs)]
    swap = [(0, 1), (1, 0)]
    grads = grad_parts.reshape(zs, 2, held, rows, cols)

    row_owner = lax.dynamic_index_in_dim(
        owners.reshape(mp, 2 * zs, held), dp, 1, keepdims=False
    ).reshape(mp * held)
    pos = jnp.arange(mp * held, dtype=jnp.int32)
    same = (row_owner[:, None] == row_owner[None, :]) & (pos[None, :] < pos[:, None])
    row_slot = jnp.sum(same.astype(jnp.int32), axis=1)
    key = row_owner * slots + row_slot
    keys = jnp.arange(mp * slots, dtype=jnp.int32)
    hit = keys[:, None] == key[None, :]
    source = jnp.sum(jnp.where(hit, pos[None, :] + 1, 0), axis=1) - 1

    other = [
        lax.ppermute(
            lax.dynamic_slice(
                grads, (0, 1 - core, j, 0, 0), (zs, 1, 1, rows, cols)
            ).reshape(zs, rows, cols),
            "core",
            swap,
        )
        for j in range(held)
    ]

    def base(step, j):
        at = (z + step) % zs
        mine = lax.dynamic_slice(grads, (at, core, j, 0, 0), (1, 1, 1, rows, cols))
        theirs = lax.dynamic_slice(other[j], (at, 0, 0), (1, rows, cols))
        return mine.reshape(rows, cols).astype(F32) + theirs.reshape(rows, cols).astype(F32)

    far = zs // 2
    left = [[far - (j % 2 == 1), far - (j % 2 == 0)] for j in range(held)]
    moving = [
        [base(left[j][0], j).astype(BF16), base(-left[j][1], j).astype(BF16)] for j in range(held)
    ]
    ended = [[None, None] for _ in range(held)]
    for _ in range(far):
        for j in range(held):
            for way in range(2):
                if left[j][way] == 0:
                    continue
                came = lax.ppermute(moving[j][way], "z", up if way == 0 else down)
                left[j][way] -= 1
                if left[j][way] == 0:
                    ended[j][way] = came
                else:
                    step = left[j][way] if way == 0 else -left[j][way]
                    moving[j][way] = (came.astype(F32) + base(step, j)).astype(BF16)
    blocks = jnp.stack(
        [
            (ended[j][0].astype(F32) + ended[j][1].astype(F32) + base(0, j))
            .astype(BF16)
            .reshape(mp, piece, cols)
            for j in range(held)
        ],
        axis=1,
    )

    sliced = lax.all_to_all(blocks, "mp", 0, 0, tiled=True)
    to_owner = pick(source, sliced.reshape(mp * held, piece, cols), mp * slots)
    own = lax.all_to_all(to_owner.reshape(mp, slots, piece, cols), "mp", 0, 0, tiled=True)
    result = precondition(own, left_root[0, 0], right_root[0, 0])
    back = lax.all_to_all(result, "mp", 0, 0, tiled=True)
    to_holder = pick(key, back.reshape(mp * slots, piece, cols), mp * held)
    home = lax.all_to_all(to_holder.reshape(mp, held, piece, cols), "mp", 0, 0, tiled=True)

    owned = own.swapaxes(0, 1).reshape(slots, rows, cols)
    left_updated = left_stats[0, 0] + jnp.einsum(
        "sik,sjk->sij", owned, owned, preferred_element_type=F32
    )
    right_updated = right_stats[0, 0] + jnp.einsum(
        "ski,skj->sij", owned, owned, preferred_element_type=F32
    )

    direction = jnp.zeros((zs, 2, held, rows, cols), BF16)

    def place(direction, value, other_value, step, j):
        at = (z + step) % zs
        for where, val in ((core, value), (1 - core, other_value)):
            direction = lax.dynamic_update_slice(
                direction, val.reshape(1, 1, 1, rows, cols), (at, where, j, 0, 0)
            )
        return direction

    mine = [home[:, j].reshape(rows, cols) for j in range(held)]
    moving = [[mine[j], mine[j]] for j in range(held)]
    for j in range(held):
        direction = place(direction, mine[j], lax.ppermute(mine[j], "core", swap), 0, j)
    for step in range(1, far + 1):
        for j in range(held):
            for way in range(2):
                if step == far and way != j % 2:
                    continue
                moving[j][way] = lax.ppermute(moving[j][way], "z", up if way == 0 else down)
                direction = place(
                    direction,
                    moving[j][way],
                    lax.ppermute(moving[j][way], "core", swap),
                    -step if way == 0 else step,
                    j,
                )
    return (
        direction.reshape(per_shard, rows, cols),
        left_updated[None, None],
        right_updated[None, None],
    )


def solution(mesh):
    split = Mesh(mesh.devices.reshape(-1, 2, mesh.shape["mp"]), ("z", "core", "mp"))
    held = P(DP, "mp", None, None, None)
    in_specs = (P(DP, "mp", None, None), held, held, held, held, P())
    out_specs = (P("mp", None, None), held, held)
    return jax.shard_map(
        per_device, mesh=split, in_specs=in_specs, out_specs=out_specs, check_vma=False
    )
```

```python
import jax
import jax.numpy as jnp
from jax import lax
from jax.experimental import pallas as pl
from jax.experimental.pallas import tpu as pltpu
from jax.sharding import Mesh
from jax.sharding import PartitionSpec as P

DP = ("z", "core")
F32 = jnp.float32
BF16 = jnp.bfloat16
SMEM = pl.BlockSpec(memory_space=pltpu.SMEM)
VMEM = pl.BlockSpec(memory_space=pltpu.VMEM)
ANYWHERE = pl.BlockSpec(memory_space=pl.ANY)


def tie(value, *others):
    return lax.optimization_barrier((value, others))[0]


def pick_kernel(source_ref, value_ref, out_ref):
    def one(i, carry):
        source = source_ref[i]
        piece = value_ref[jnp.maximum(source, 0)]
        out_ref[i] = jnp.where(source >= 0, piece, jnp.zeros_like(piece))
        return carry

    lax.fori_loop(0, out_ref.shape[0], one, 0, unroll=8)


def pick(source, values):
    return pl.pallas_call(
        pick_kernel,
        out_shape=jax.ShapeDtypeStruct((*source.shape, *values.shape[1:]), values.dtype),
        in_specs=[SMEM, VMEM],
        out_specs=VMEM,
        name="pick",
    )(source, values)


def precond_kernel(grad_ref, root_ref, out_ref):
    held, rows, cols = grad_ref.shape
    for j in range(held):
        left = root_ref[:, j, 0].reshape(rows, rows)
        right = root_ref[:, j, 1].reshape(cols, cols)
        half = jnp.dot(left, grad_ref[j], preferred_element_type=F32).astype(BF16)
        out_ref[j] = jnp.dot(half, right, preferred_element_type=F32).astype(BF16)


def precondition(grads, roots):
    return pl.pallas_call(
        precond_kernel,
        out_shape=jax.ShapeDtypeStruct(grads.shape, BF16),
        in_specs=[VMEM, VMEM],
        out_specs=VMEM,
        name="precondition",
    )(grads, roots)


def statistics_kernel(own_ref, left_ref, right_ref, left_out_ref, right_out_ref):
    peers, _, piece, cols = own_ref.shape
    own = own_ref[:, 0].reshape(peers * piece, cols)
    left_out_ref[0] = left_ref[0] + lax.dot_general(
        own, own, (((1,), (1,)), ((), ())), preferred_element_type=F32
    )
    right_out_ref[0] = right_ref[0] + lax.dot_general(
        own, own, (((0,), (0,)), ((), ())), preferred_element_type=F32
    )


def statistics(own, left, right):
    peers, slots, piece, cols = own.shape
    one = pl.BlockSpec((1, *left.shape[1:]), lambda s: (s, 0, 0))
    return pl.pallas_call(
        statistics_kernel,
        grid=(slots,),
        out_shape=(
            jax.ShapeDtypeStruct(left.shape, F32),
            jax.ShapeDtypeStruct(right.shape, F32),
        ),
        in_specs=[pl.BlockSpec((peers, 1, piece, cols), lambda s: (0, s, 0, 0)), one, one],
        out_specs=(one, one),
        name="statistics",
    )(own, left, right)


def place(where, pieces, direction, shape):
    zs = shape[0]
    fresh = direction is None

    def kernel(where_ref, *refs):
        refs = list(refs)
        sem = refs.pop()
        out_ref = refs.pop()
        if not fresh:
            refs.pop(0)
        z, core = where_ref[0], where_ref[1]
        way = 1 - 2 * core
        copies = []
        for ref, (places, value) in zip(refs, pieces):
            for i, (step, cross, part) in enumerate(places):
                at = lax.rem(z + way * step + zs, zs)
                side = 1 - core if cross else core
                target = out_ref.at[at, side]
                if part is not None:
                    target = target.at[pl.ds(1 - core if part else core, 1)]
                copies.append(pltpu.make_async_copy(ref.at[i], target, sem.at[len(copies)]))
        for copy in copies:
            copy.start()
        for copy in copies:
            copy.wait()

    operands = ([] if fresh else [direction]) + [value for _, value in pieces]
    return pl.pallas_call(
        kernel,
        out_shape=jax.ShapeDtypeStruct(shape, BF16),
        in_specs=[SMEM] + ([] if fresh else [ANYWHERE]) + [VMEM] * len(pieces),
        out_specs=ANYWHERE,
        scratch_shapes=[pltpu.SemaphoreType.DMA((sum(len(p) for p, _ in pieces),))],
        input_output_aliases={} if fresh else {1: 0},
        name="place",
    )(where, *operands)


def per_device(grad_parts, left_stats, right_stats, left_root, right_root, owners):
    zs = lax.axis_size("z")
    mp = lax.axis_size("mp")
    z = lax.axis_index("z")
    core = lax.axis_index("core")
    way = 1 - 2 * core
    dp = z * 2 + core
    _, per_shard, rows, cols = grad_parts.shape
    held = per_shard // (2 * zs)
    slots = left_stats.shape[2]
    piece = rows // mp
    far = zs // 2
    grads = grad_parts.reshape(zs, 2, held, rows, cols)
    ring = [(2 * i, 2 * ((i + 1) % zs)) for i in range(zs)]
    ring += [(2 * i + 1, 2 * ((i - 1) % zs) + 1) for i in range(zs)]

    def hop(value):
        return lax.ppermute(value, DP, ring)

    def swap(value):
        return lax.ppermute(value, "core", [(0, 1), (1, 0)])

    row_owner = lax.dynamic_slice(
        owners.reshape(mp, 2 * zs, held), (0, dp, 0), (mp, 1, held)
    ).reshape(mp * held)
    pos = jnp.arange(mp * held, dtype=jnp.int32)
    same = (row_owner[:, None] == row_owner[None, :]) & (pos[None, :] < pos[:, None])
    key = row_owner * slots + jnp.sum(same.astype(jnp.int32), axis=1)
    keys = jnp.arange(mp * slots, dtype=jnp.int32)
    hit = keys[:, None] == key[None, :]
    source = jnp.sum(jnp.where(hit, pos[None, :] + 1, 0), axis=1) - 1

    def rows_for(step, part):
        at = (z + step + zs) % zs
        if part is None:
            return lax.dynamic_slice(
                grads, (at, 0, 0, 0, 0), (1, 2, held, rows, cols)
            ).reshape(2, held, rows, cols)
        return lax.dynamic_slice(
            grads, (at, 0, part, 0, 0), (1, 2, 1, rows, cols)
        ).reshape(2, 1, rows, cols)

    def base(step, theirs, part=None):
        return rows_for(way * step, part).astype(F32) + theirs.astype(F32)

    theirs = swap(rows_for(-way * far, 1 - core))
    theirs3 = swap(rows_for(-way * (far - 1), None))
    moving = base(far, theirs, core).astype(BF16)
    came = hop(moving)

    spread = jnp.stack([left_root[0, 0], right_root[0, 0]], axis=1).reshape(
        slots, 2, mp, piece, cols
    )
    spread = tie(jnp.moveaxis(spread, 2, 0), moving)
    spread = lax.all_to_all(spread, "mp", 0, 0, tiled=True)
    wanted = pick(key, spread.reshape(mp * slots, 2, piece, cols))
    roots = lax.all_to_all(wanted.reshape(mp, held, 2, piece, cols), "mp", 0, 0, tiled=True)

    nearer = base(far - 1, tie(theirs3, moving))
    mine = jnp.where(
        jnp.arange(held)[None, :, None, None] == core,
        jnp.broadcast_to(came, nearer.shape).astype(F32),
        0,
    )
    for step in range(far - 1, 0, -1):
        before = moving
        moving = (mine + nearer).astype(BF16)
        came = hop(moving)
        if step > 1:
            theirs = swap(tie(rows_for(-way * (step - 1), None), before))
            nearer = lax.optimization_barrier(base(step - 1, tie(theirs, moving)))
            mine = came.astype(F32)

    def side(value, which):
        return lax.dynamic_slice(value, (which, 0, 0, 0), (1, held, rows, cols))[0]

    here = lax.dynamic_slice(grads, (z, 0, 0, 0, 0), (1, 2, held, rows, cols))[0]
    give = (side(came, 1 - core).astype(F32) + side(here, 1 - core).astype(F32)).astype(BF16)
    taken = swap(give)
    blocks = (
        side(came, core).astype(F32) + side(here, core).astype(F32) + taken.astype(F32)
    ).astype(BF16)

    result = precondition(blocks, roots)

    sliced = jnp.moveaxis(tie(blocks, result).reshape(held, mp, piece, cols), 1, 0)
    sliced = lax.all_to_all(sliced, "mp", 0, 0, tiled=True)
    to_owner = pick(source, sliced.reshape(mp * held, piece, cols))
    own = lax.all_to_all(to_owner.reshape(mp, slots, piece, cols), "mp", 0, 0, tiled=True)
    left_updated, right_updated = statistics(own, left_stats[0, 0], right_stats[0, 0])

    shape = (zs, 2, held, rows, cols)
    where = jnp.stack([z, core])
    beside = swap(result)
    pieces = [([(0, False, None)], result[None]), ([(0, True, None)], beside[None])]
    flow = [result, beside]
    for step in range(1, far):
        flow = [hop(value) for value in flow]
        pair = jnp.stack(flow)
        got = swap(pair)
        pieces.append(([(-step, False, None), (-step, True, None)], pair))
        pieces.append(([(step, True, None), (step, False, None)], got))
    flow = [
        hop(lax.dynamic_slice(value, (core, 0, 0), (1, rows, cols))) for value in flow
    ]
    pair = jnp.stack(flow)
    got = swap(pair)
    late = [([(far, False, 0), (far, True, 0)], pair), ([(far, True, 1), (far, False, 1)], got)]
    direction = place(where, pieces, None, shape)
    direction = place(where, late, direction, shape)
    return (
        direction.reshape(per_shard, rows, cols),
        left_updated[None, None],
        right_updated[None, None],
    )


def solution(mesh):
    split = Mesh(mesh.devices.reshape(-1, 2, mesh.shape["mp"]), ("z", "core", "mp"))
    held = P(DP, "mp", None, None, None)
    in_specs = (P(DP, "mp", None, None), held, held, held, held, P())
    out_specs = (P("mp", None, None), held, held)
    return jax.shard_map(
        per_device, mesh=split, in_specs=in_specs, out_specs=out_specs, check_vma=False
    )
```

```python
import jax
import jax.numpy as jnp
from jax import lax
from jax.experimental import pallas as pl
from jax.experimental.pallas import tpu as pltpu
from jax.sharding import Mesh
from jax.sharding import PartitionSpec as P

DP = ("z", "core")
F32 = jnp.float32
BF16 = jnp.bfloat16
SMEM = pl.BlockSpec(memory_space=pltpu.SMEM)
VMEM = pl.BlockSpec(memory_space=pltpu.VMEM)
ANYWHERE = pl.BlockSpec(memory_space=pl.ANY)


def tie(value, *others):
    return lax.optimization_barrier((value, others))[0]


def pick_kernel(source_ref, value_ref, out_ref):
    def one(i, carry):
        source = source_ref[i]
        piece = value_ref[jnp.maximum(source, 0)]
        out_ref[i] = jnp.where(source >= 0, piece, jnp.zeros_like(piece))
        return carry

    lax.fori_loop(0, out_ref.shape[0], one, 0, unroll=8)


def pick(source, values):
    return pl.pallas_call(
        pick_kernel,
        out_shape=jax.ShapeDtypeStruct((*source.shape, *values.shape[1:]), values.dtype),
        in_specs=[SMEM, VMEM],
        out_specs=VMEM,
        name="pick",
    )(source, values)


def precond_kernel(grad_ref, root_ref, out_ref):
    held, rows, cols = grad_ref.shape
    for j in range(held):
        left = root_ref[:, j, 0].reshape(rows, rows)
        right = root_ref[:, j, 1].reshape(cols, cols)
        half = jnp.dot(left, grad_ref[j], preferred_element_type=F32).astype(BF16)
        out_ref[j] = jnp.dot(half, right, preferred_element_type=F32).astype(BF16)


def precondition(grads, roots):
    return pl.pallas_call(
        precond_kernel,
        out_shape=jax.ShapeDtypeStruct(grads.shape, BF16),
        in_specs=[VMEM, VMEM],
        out_specs=VMEM,
        name="precondition",
    )(grads, roots)


def statistics_kernel(own_ref, left_ref, right_ref, left_out_ref, right_out_ref):
    peers, _, piece, cols = own_ref.shape
    own = own_ref[:, 0].reshape(peers * piece, cols)
    left_out_ref[0] = left_ref[0] + lax.dot_general(
        own, own, (((1,), (1,)), ((), ())), preferred_element_type=F32
    )
    right_out_ref[0] = right_ref[0] + lax.dot_general(
        own, own, (((0,), (0,)), ((), ())), preferred_element_type=F32
    )


def statistics(own, left, right):
    peers, slots, piece, cols = own.shape
    one = pl.BlockSpec((1, *left.shape[1:]), lambda s: (s, 0, 0))
    return pl.pallas_call(
        statistics_kernel,
        grid=(slots,),
        out_shape=(
            jax.ShapeDtypeStruct(left.shape, F32),
            jax.ShapeDtypeStruct(right.shape, F32),
        ),
        in_specs=[pl.BlockSpec((peers, 1, piece, cols), lambda s: (0, s, 0, 0)), one, one],
        out_specs=(one, one),
        name="statistics",
    )(own, left, right)


def place(where, pieces, direction, shape):
    zs = shape[0]
    fresh = direction is None

    def kernel(where_ref, *refs):
        refs = list(refs)
        sem = refs.pop()
        out_ref = refs.pop()
        if not fresh:
            refs.pop(0)
        z, core = where_ref[0], where_ref[1]
        copies = []
        for ref, (places, value) in zip(refs, pieces):
            for i, (step, cross, part) in enumerate(places):
                at = lax.rem(z + step + zs, zs)
                side = 1 - core if cross else core
                target = out_ref.at[at, side]
                if part is not None:
                    target = target.at[pl.ds(part, 1)]
                copies.append(pltpu.make_async_copy(ref.at[i], target, sem.at[len(copies)]))
        for copy in copies:
            copy.start()
        for copy in copies:
            copy.wait()

    operands = ([] if fresh else [direction]) + [value for _, value in pieces]
    return pl.pallas_call(
        kernel,
        out_shape=jax.ShapeDtypeStruct(shape, BF16),
        in_specs=[SMEM] + ([] if fresh else [ANYWHERE]) + [VMEM] * len(pieces),
        out_specs=ANYWHERE,
        scratch_shapes=[pltpu.SemaphoreType.DMA((sum(len(p) for p, _ in pieces),))],
        input_output_aliases={} if fresh else {1: 0},
        name="place",
    )(where, *operands)


def per_device(grad_parts, left_stats, right_stats, left_root, right_root, owners):
    zs = lax.axis_size("z")
    mp = lax.axis_size("mp")
    z = lax.axis_index("z")
    core = lax.axis_index("core")
    dp = z * 2 + core
    _, per_shard, rows, cols = grad_parts.shape
    held = per_shard // (2 * zs)
    slots = left_stats.shape[2]
    piece = rows // mp
    far = zs // 2
    grads = grad_parts.reshape(zs, 2, held, rows, cols)
    ways = [[(i, (i + 1) % zs) for i in range(zs)], [(i, (i - 1) % zs) for i in range(zs)]]

    def hop(value, way):
        return lax.ppermute(value, "z", ways[way])

    def swap(value):
        return lax.ppermute(value, "core", [(0, 1), (1, 0)])

    row_owner = lax.dynamic_slice(
        owners.reshape(mp, 2 * zs, held), (0, dp, 0), (mp, 1, held)
    ).reshape(mp * held)
    pos = jnp.arange(mp * held, dtype=jnp.int32)
    same = (row_owner[:, None] == row_owner[None, :]) & (pos[None, :] < pos[:, None])
    key = row_owner * slots + jnp.sum(same.astype(jnp.int32), axis=1)
    keys = jnp.arange(mp * slots, dtype=jnp.int32)
    hit = keys[:, None] == key[None, :]
    source = jnp.sum(jnp.where(hit, pos[None, :] + 1, 0), axis=1) - 1

    def rows_of(step, which):
        at = (z + step + zs) % zs
        return lax.dynamic_slice(
            grads, (at, which, 0, 0, 0), (1, 1, held, rows, cols)
        ).reshape(held, rows, cols)

    def base(step, *others):
        at = (z + step + zs) % zs
        at = tie(at, *others) if others else at
        given = lax.dynamic_slice(theirs, (at, 0, 0, 0), (1, held, rows, cols))[0]
        mine = lax.dynamic_slice(grads, (at, core, 0, 0, 0), (1, 1, held, rows, cols))
        value = mine.reshape(held, rows, cols).astype(F32) + given.astype(F32)
        return lax.optimization_barrier(value)

    farthest = swap(rows_of(far, 1 - core))
    theirs = lax.dynamic_slice(
        grads, (0, 1 - core, 0, 0, 0), (zs, 1, held, rows, cols)
    ).reshape(zs, held, rows, cols)
    moving = rows_of(far, core)
    moving = [
        (moving[way : way + 1].astype(F32) + farthest[way : way + 1].astype(F32)).astype(BF16)
        for way in range(2)
    ]
    theirs = swap(tie(theirs, *moving))
    came = [hop(moving[way], way) for way in range(2)]

    spread = jnp.stack([left_root[0, 0], right_root[0, 0]], axis=1).reshape(
        slots, 2, mp, piece, cols
    )
    spread = jnp.moveaxis(tie(spread, *moving), 2, 0)
    spread = lax.all_to_all(spread, "mp", 0, 0, tiled=True)

    first = jnp.arange(held)[:, None, None]
    came = [
        jnp.where(first == way, jnp.broadcast_to(came[way], (held, rows, cols)).astype(F32), 0)
        for way in range(2)
    ]
    for step in range(far - 1, 0, -1):
        added = [base(step, *moving), base(-step, *moving)]
        moving = [(came[way].astype(F32) + added[way]).astype(BF16) for way in range(2)]
        if step == far - 2:
            wanted = pick(key, tie(spread, *moving).reshape(mp * slots, 2, piece, cols))
            wanted = wanted.reshape(mp, held, 2, piece, cols)
            roots = lax.all_to_all(wanted, "mp", 0, 0, tiled=True)
        came = [hop(moving[way], way) for way in range(2)]
    blocks = (
        came[0].astype(F32) + came[1].astype(F32) + base(0, *moving)
    ).astype(BF16)

    sliced = jnp.moveaxis(blocks.reshape(held, mp, piece, cols), 1, 0)
    result = precondition(tie(blocks, sliced), roots)

    arrived = lax.all_to_all(sliced, "mp", 0, 0, tiled=True)

    shape = (zs, 2, held, rows, cols)
    where = jnp.stack([z, core])
    pieces = [([(0, False, None)], result[None]), ([(0, True, None)], swap(result)[None])]
    flow = [result, result]
    for step in range(1, far):
        flow = [hop(flow[way], way) for way in range(2)]
        if step == far - 2:
            flow = tie(flow, to_owner)
        if step == far - 1:
            flow = tie(flow, own)
        if step == far - 3:
            to_owner = pick(source, tie(arrived, *flow).reshape(mp * held, piece, cols))
            own = lax.all_to_all(
                to_owner.reshape(mp, slots, piece, cols), "mp", 0, 0, tiled=True
            )
        pair = jnp.stack(flow)
        for cross, value in ((False, pair), (True, swap(pair))):
            pieces.append(([(-step, cross, None), (step, cross, None)], value))
    flow = [hop(flow[way][way : way + 1], way) for way in range(2)]
    left_updated, right_updated = statistics(own, left_stats[0, 0], right_stats[0, 0])
    direction = place(tie(where, left_updated), pieces, None, shape)
    pair = jnp.stack(tie(flow, direction))
    late = [
        ([(-far, cross, 0), (far, cross, 1)], value)
        for cross, value in ((False, pair), (True, swap(pair)))
    ]
    direction = place(where, late, direction, shape)
    return (
        direction.reshape(per_shard, rows, cols),
        left_updated[None, None],
        right_updated[None, None],
    )


def solution(mesh):
    split = Mesh(mesh.devices.reshape(-1, 2, mesh.shape["mp"]), ("z", "core", "mp"))
    held = P(DP, "mp", None, None, None)
    in_specs = (P(DP, "mp", None, None), held, held, held, held, P())
    out_specs = (P("mp", None, None), held, held)
    return jax.shard_map(
        per_device, mesh=split, in_specs=in_specs, out_specs=out_specs, check_vma=False
    )
```

```python
import jax
import jax.numpy as jnp
from jax import lax
from jax.experimental import pallas as pl
from jax.experimental.pallas import tpu as pltpu
from jax.sharding import Mesh
from jax.sharding import PartitionSpec as P

DP = ("z", "core")
F32 = jnp.float32
BF16 = jnp.bfloat16
SMEM = pl.BlockSpec(memory_space=pltpu.SMEM)
VMEM = pl.BlockSpec(memory_space=pltpu.VMEM)
ANYWHERE = pl.BlockSpec(memory_space=pl.ANY)
LIMIT = pltpu.CompilerParams(vmem_limit_bytes=12 * 2**20)


def near(value):
    return pltpu.with_memory_space_constraint(value, pltpu.VMEM)


def tie(value, *others):
    return lax.optimization_barrier((value, others))[0]


def pick_kernel(source_ref, value_ref, out_ref):
    def one(i, carry):
        source = source_ref[i]
        piece = value_ref[jnp.maximum(source, 0)]
        out_ref[i] = jnp.where(source >= 0, piece, jnp.zeros_like(piece))
        return carry

    lax.fori_loop(0, out_ref.shape[0], one, 0, unroll=8)


def pick(source, values):
    return pl.pallas_call(
        pick_kernel,
        out_shape=jax.ShapeDtypeStruct((*source.shape, *values.shape[1:]), values.dtype),
        in_specs=[SMEM, VMEM],
        out_specs=VMEM,
        compiler_params=LIMIT,
        name="pick",
    )(source, near(values))


def precond_kernel(grad_ref, root_ref, out_ref):
    held, rows, cols = grad_ref.shape
    for j in range(held):
        left = root_ref[:, j, 0].reshape(rows, rows)
        right = root_ref[:, j, 1].reshape(cols, cols)
        half = jnp.dot(left, grad_ref[j], preferred_element_type=F32).astype(BF16)
        out_ref[j] = jnp.dot(half, right, preferred_element_type=F32).astype(BF16)


def precondition(grads, roots):
    return pl.pallas_call(
        precond_kernel,
        out_shape=jax.ShapeDtypeStruct(grads.shape, BF16),
        in_specs=[VMEM, VMEM],
        out_specs=VMEM,
        compiler_params=LIMIT,
        name="precondition",
    )(near(grads), near(roots))


def statistics_kernel(own_ref, left_ref, right_ref, left_out_ref, right_out_ref):
    peers, _, piece, cols = own_ref.shape
    own = own_ref[:, pl.program_id(0)].reshape(peers * piece, cols)
    left_out_ref[0] = left_ref[0] + lax.dot_general(
        own, own, (((1,), (1,)), ((), ())), preferred_element_type=F32
    )
    right_out_ref[0] = right_ref[0] + lax.dot_general(
        own, own, (((0,), (0,)), ((), ())), preferred_element_type=F32
    )


def statistics(own, left, right):
    slots = own.shape[1]
    one = pl.BlockSpec((1, *left.shape[1:]), lambda s: (s, 0, 0))
    return pl.pallas_call(
        statistics_kernel,
        grid=(slots,),
        out_shape=(
            jax.ShapeDtypeStruct(left.shape, F32),
            jax.ShapeDtypeStruct(right.shape, F32),
        ),
        in_specs=[VMEM, one, one],
        out_specs=(one, one),
        compiler_params=LIMIT,
        name="statistics",
    )(near(own), left, right)


def place(where, pieces, direction, shape):
    zs = shape[0]
    fresh = direction is None

    def kernel(where_ref, *refs):
        refs = list(refs)
        sem = refs.pop()
        out_ref = refs.pop()
        if not fresh:
            refs.pop(0)
        z, core = where_ref[0], where_ref[1]
        copies = []
        for ref, (places, value) in zip(refs, pieces):
            for i, (step, cross, part) in enumerate(places):
                at = lax.rem(z + step + zs, zs)
                side = 1 - core if cross else core
                target = out_ref.at[at, side]
                if part is not None:
                    target = target.at[pl.ds(part, 1)]
                copies.append(pltpu.make_async_copy(ref.at[i], target, sem.at[len(copies)]))
        for copy in copies:
            copy.start()
        for copy in copies:
            copy.wait()

    operands = ([] if fresh else [direction]) + [near(value) for _, value in pieces]
    return pl.pallas_call(
        kernel,
        out_shape=jax.ShapeDtypeStruct(shape, BF16),
        in_specs=[SMEM] + ([] if fresh else [ANYWHERE]) + [VMEM] * len(pieces),
        out_specs=ANYWHERE,
        scratch_shapes=[pltpu.SemaphoreType.DMA((sum(len(p) for p, _ in pieces),))],
        input_output_aliases={} if fresh else {1: 0},
        compiler_params=LIMIT,
        name="place",
    )(where, *operands)


def per_device(grad_parts, left_stats, right_stats, left_root, right_root, owners):
    zs = lax.axis_size("z")
    mp = lax.axis_size("mp")
    z = lax.axis_index("z")
    core = lax.axis_index("core")
    dp = z * 2 + core
    _, per_shard, rows, cols = grad_parts.shape
    held = per_shard // (2 * zs)
    slots = left_stats.shape[2]
    piece = rows // mp
    far = zs // 2
    grads = grad_parts.reshape(zs, 2, held, rows, cols)
    ways = [[(i, (i + 1) % zs) for i in range(zs)], [(i, (i - 1) % zs) for i in range(zs)]]

    def hop(value, way):
        return lax.ppermute(value, "z", ways[way])

    def swap(value):
        return lax.ppermute(value, "core", [(0, 1), (1, 0)])

    row_owner = lax.dynamic_slice(
        owners.reshape(mp, 2 * zs, held), (0, dp, 0), (mp, 1, held)
    ).reshape(mp * held)
    pos = jnp.arange(mp * held, dtype=jnp.int32)
    same = (row_owner[:, None] == row_owner[None, :]) & (pos[None, :] < pos[:, None])
    key = row_owner * slots + jnp.sum(same.astype(jnp.int32), axis=1)
    keys = jnp.arange(mp * slots, dtype=jnp.int32)
    hit = keys[:, None] == key[None, :]
    source = jnp.sum(jnp.where(hit, pos[None, :] + 1, 0), axis=1) - 1

    def rows_of(step, which):
        at = (z + step + zs) % zs
        return lax.dynamic_slice(
            grads, (at, which, 0, 0, 0), (1, 1, held, rows, cols)
        ).reshape(held, rows, cols)

    def base(step, *others):
        at = (z + step + zs) % zs
        at = tie(at, *others) if others else at
        given = lax.dynamic_slice(theirs, (at, 0, 0, 0), (1, held, rows, cols))[0]
        mine = lax.dynamic_slice(grads, (at, core, 0, 0, 0), (1, 1, held, rows, cols))
        value = mine.reshape(held, rows, cols).astype(F32) + given.astype(F32)
        return lax.optimization_barrier(value)

    farthest = swap(rows_of(far, 1 - core))
    theirs = lax.dynamic_slice(
        grads, (0, 1 - core, 0, 0, 0), (zs, 1, held, rows, cols)
    ).reshape(zs, held, rows, cols)
    moving = rows_of(far, core)
    moving = [
        (moving[way : way + 1].astype(F32) + farthest[way : way + 1].astype(F32)).astype(BF16)
        for way in range(2)
    ]
    theirs = swap(tie(theirs, *moving))
    came = [hop(moving[way], way) for way in range(2)]

    spread = jnp.stack([left_root[0, 0], right_root[0, 0]], axis=1).reshape(
        slots, 2, mp, piece, cols
    )
    spread = jnp.moveaxis(tie(spread, *moving), 2, 0)
    spread = lax.all_to_all(spread, "mp", 0, 0, tiled=True)

    first = jnp.arange(held)[:, None, None]
    came = [
        jnp.where(first == way, jnp.broadcast_to(came[way], (held, rows, cols)).astype(F32), 0)
        for way in range(2)
    ]
    for step in range(far - 1, 0, -1):
        added = [base(step, *moving), base(-step, *moving)]
        moving = [(came[way].astype(F32) + added[way]).astype(BF16) for way in range(2)]
        if step == far - 2:
            wanted = pick(key, tie(spread, *moving).reshape(mp * slots, 2, piece, cols))
            wanted = wanted.reshape(mp, held, 2, piece, cols)
            roots = lax.all_to_all(wanted, "mp", 0, 0, tiled=True)
        came = [hop(moving[way], way) for way in range(2)]
    blocks = (
        came[0].astype(F32) + came[1].astype(F32) + base(0, *moving, roots)
    ).astype(BF16)

    sliced = jnp.moveaxis(blocks.reshape(held, mp, piece, cols), 1, 0)
    result = precondition(tie(blocks, sliced), roots)

    arrived = lax.all_to_all(sliced, "mp", 0, 0, tiled=True)

    shape = (zs, 2, held, rows, cols)
    where = jnp.stack([z, core])
    pieces = [([(0, False, None)], result[None]), ([(0, True, None)], swap(result)[None])]
    flow = [result, result]
    for step in range(1, far):
        flow = [hop(flow[way], way) for way in range(2)]
        if step == far - 2:
            flow = tie(flow, to_owner)
        if step == far - 1:
            flow = tie(flow, own)
        if step == far - 3:
            to_owner = pick(source, tie(arrived, *flow).reshape(mp * held, piece, cols))
            own = lax.all_to_all(
                to_owner.reshape(mp, slots, piece, cols), "mp", 0, 0, tiled=True
            )
        pair = jnp.stack(flow)
        for cross, value in ((False, pair), (True, swap(pair))):
            pieces.append(([(-step, cross, None), (step, cross, None)], value))
    flow = [hop(flow[way][way : way + 1], way) for way in range(2)]
    left_updated, right_updated = statistics(own, left_stats[0, 0], right_stats[0, 0])
    direction = place(tie(where, left_updated), pieces, None, shape)
    pair = jnp.stack(tie(flow, direction))
    late = [
        ([(-far, cross, 0), (far, cross, 1)], value)
        for cross, value in ((False, pair), (True, swap(pair)))
    ]
    direction = place(where, late, direction, shape)
    return (
        direction.reshape(per_shard, rows, cols),
        left_updated[None, None],
        right_updated[None, None],
    )


def solution(mesh):
    split = Mesh(mesh.devices.reshape(-1, 2, mesh.shape["mp"]), ("z", "core", "mp"))
    held = P(DP, "mp", None, None, None)
    in_specs = (P(DP, "mp", None, None), held, held, held, held, P())
    out_specs = (P("mp", None, None), held, held)
    return jax.shard_map(
        per_device, mesh=split, in_specs=in_specs, out_specs=out_specs, check_vma=False
    )
```

```python
import jax
import jax.numpy as jnp
from jax import lax
from jax.experimental import pallas as pl
from jax.experimental.pallas import tpu as pltpu
from jax.sharding import Mesh
from jax.sharding import PartitionSpec as P

DP = ("z", "core")
F32 = jnp.float32
BF16 = jnp.bfloat16
SMEM = pl.BlockSpec(memory_space=pltpu.SMEM)
VMEM = pl.BlockSpec(memory_space=pltpu.VMEM)
ANYWHERE = pl.BlockSpec(memory_space=pl.ANY)
LIMIT = pltpu.CompilerParams(vmem_limit_bytes=12 * 2**20)


def near(value):
    return pltpu.with_memory_space_constraint(value, pltpu.VMEM)


def tie(value, *others):
    return lax.optimization_barrier((value, others))[0]


def pick_kernel(source_ref, value_ref, out_ref):
    def one(i, carry):
        source = source_ref[i]
        piece = value_ref[jnp.maximum(source, 0)]
        out_ref[i] = jnp.where(source >= 0, piece, jnp.zeros_like(piece))
        return carry

    lax.fori_loop(0, out_ref.shape[0], one, 0, unroll=8)


def pick(source, values):
    return pl.pallas_call(
        pick_kernel,
        out_shape=jax.ShapeDtypeStruct((*source.shape, *values.shape[1:]), values.dtype),
        in_specs=[SMEM, VMEM],
        out_specs=VMEM,
        compiler_params=LIMIT,
        name="pick",
    )(source, near(values))


def precond_kernel(grad_ref, root_ref, out_ref, sliced_ref):
    held, rows, cols = grad_ref.shape
    for j in range(held):
        left = root_ref[:, j, 0].reshape(rows, rows)
        right = root_ref[:, j, 1].reshape(cols, cols)
        half = jnp.dot(left, grad_ref[j], preferred_element_type=F32).astype(BF16)
        out_ref[j] = jnp.dot(half, right, preferred_element_type=F32).astype(BF16)
        sliced_ref[:, j] = grad_ref[j].reshape(sliced_ref.shape[0], *sliced_ref.shape[2:])


def precondition(grads, roots):
    held, rows, cols = grads.shape
    peers = roots.shape[0]
    return pl.pallas_call(
        precond_kernel,
        out_shape=(
            jax.ShapeDtypeStruct(grads.shape, BF16),
            jax.ShapeDtypeStruct((peers, held, rows // peers, cols), BF16),
        ),
        in_specs=[VMEM, VMEM],
        out_specs=(VMEM, VMEM),
        compiler_params=LIMIT,
        name="precondition",
    )(near(grads), near(roots))


def part_kernel(up_ref, down_ref, up_part_ref, down_part_ref, pair_ref):
    up_part_ref[...] = up_ref[0:1]
    down_part_ref[...] = down_ref[1:2]
    pair_ref[0] = up_ref[...]
    pair_ref[1] = down_ref[...]


def part(up, down):
    one = jax.ShapeDtypeStruct((1, *up.shape[1:]), BF16)
    return pl.pallas_call(
        part_kernel,
        out_shape=(one, one, jax.ShapeDtypeStruct((2, *up.shape), BF16)),
        in_specs=[VMEM, VMEM],
        out_specs=(VMEM, VMEM, VMEM),
        compiler_params=LIMIT,
        name="part",
    )(near(up), near(down))


def statistics_kernel(own_ref, left_ref, right_ref, left_out_ref, right_out_ref):
    peers, _, piece, cols = own_ref.shape
    own = own_ref[:, pl.program_id(0)].reshape(peers * piece, cols)
    left_out_ref[0] = left_ref[0] + lax.dot_general(
        own, own, (((1,), (1,)), ((), ())), preferred_element_type=F32
    )
    right_out_ref[0] = right_ref[0] + lax.dot_general(
        own, own, (((0,), (0,)), ((), ())), preferred_element_type=F32
    )


def statistics(own, left, right):
    slots = own.shape[1]
    one = pl.BlockSpec((1, *left.shape[1:]), lambda s: (s, 0, 0))
    return pl.pallas_call(
        statistics_kernel,
        grid=(slots,),
        out_shape=(
            jax.ShapeDtypeStruct(left.shape, F32),
            jax.ShapeDtypeStruct(right.shape, F32),
        ),
        in_specs=[VMEM, one, one],
        out_specs=(one, one),
        compiler_params=LIMIT,
        name="statistics",
    )(near(own), *(pltpu.with_memory_space_constraint(x, pltpu.HBM) for x in (left, right)))


def place(where, pieces, direction, shape):
    zs = shape[0]
    fresh = direction is None

    def kernel(where_ref, *refs):
        refs = list(refs)
        sem = refs.pop()
        out_ref = refs.pop()
        if not fresh:
            refs.pop(0)
        z, core = where_ref[0], where_ref[1]
        copies = []
        for ref, (places, value) in zip(refs, pieces):
            for i, (step, cross, part) in enumerate(places):
                at = lax.rem(z + step + zs, zs)
                side = 1 - core if cross else core
                target = out_ref.at[at, side]
                if part is not None:
                    target = target.at[pl.ds(part, 1)]
                copies.append(pltpu.make_async_copy(ref.at[i], target, sem.at[len(copies)]))
        for copy in copies:
            copy.start()
        for copy in copies:
            copy.wait()

    operands = ([] if fresh else [direction]) + [near(value) for _, value in pieces]
    return pl.pallas_call(
        kernel,
        out_shape=jax.ShapeDtypeStruct(shape, BF16),
        in_specs=[SMEM] + ([] if fresh else [ANYWHERE]) + [VMEM] * len(pieces),
        out_specs=ANYWHERE,
        scratch_shapes=[pltpu.SemaphoreType.DMA((sum(len(p) for p, _ in pieces),))],
        input_output_aliases={} if fresh else {1: 0},
        compiler_params=LIMIT,
        name="place",
    )(where, *operands)


def per_device(grad_parts, left_stats, right_stats, left_root, right_root, owners):
    zs = lax.axis_size("z")
    mp = lax.axis_size("mp")
    z = lax.axis_index("z")
    core = lax.axis_index("core")
    dp = z * 2 + core
    _, per_shard, rows, cols = grad_parts.shape
    held = per_shard // (2 * zs)
    slots = left_stats.shape[2]
    piece = rows // mp
    far = zs // 2
    grads = grad_parts.reshape(zs, 2, held, rows, cols)
    ways = [[(i, (i + 1) % zs) for i in range(zs)], [(i, (i - 1) % zs) for i in range(zs)]]

    def hop(value, way):
        return lax.ppermute(value, "z", ways[way])

    def swap(value):
        return lax.ppermute(value, "core", [(0, 1), (1, 0)])

    row_owner = lax.dynamic_slice(
        owners.reshape(mp, 2 * zs, held), (0, dp, 0), (mp, 1, held)
    ).reshape(mp * held)
    pos = jnp.arange(mp * held, dtype=jnp.int32)
    same = (row_owner[:, None] == row_owner[None, :]) & (pos[None, :] < pos[:, None])
    key = row_owner * slots + jnp.sum(same.astype(jnp.int32), axis=1)
    keys = jnp.arange(mp * slots, dtype=jnp.int32)
    hit = keys[:, None] == key[None, :]
    source = jnp.sum(jnp.where(hit, pos[None, :] + 1, 0), axis=1) - 1

    def rows_of(step, which):
        at = (z + step + zs) % zs
        return lax.dynamic_slice(
            grads, (at, which, 0, 0, 0), (1, 1, held, rows, cols)
        ).reshape(held, rows, cols)

    def base(step, *others):
        at = (z + step + zs) % zs
        at = tie(at, *others) if others else at
        given = lax.dynamic_slice(theirs, (at, 0, 0, 0), (1, held, rows, cols))[0]
        mine = lax.dynamic_slice(grads, (at, core, 0, 0, 0), (1, 1, held, rows, cols))
        value = mine.reshape(held, rows, cols).astype(F32) + given.astype(F32)
        return lax.optimization_barrier(value)

    farthest = swap(rows_of(far, 1 - core))
    theirs = lax.dynamic_slice(
        grads, (0, 1 - core, 0, 0, 0), (zs, 1, held, rows, cols)
    ).reshape(zs, held, rows, cols)
    moving = rows_of(far, core)
    moving = [
        (moving[way : way + 1].astype(F32) + farthest[way : way + 1].astype(F32)).astype(BF16)
        for way in range(2)
    ]
    theirs = swap(tie(theirs, *moving))
    came = [hop(moving[way], way) for way in range(2)]

    spread = jnp.stack([left_root[0, 0], right_root[0, 0]], axis=1).reshape(
        slots, 2, mp, piece, cols
    )
    spread = jnp.moveaxis(tie(spread, *moving), 2, 0)
    spread = lax.all_to_all(spread, "mp", 0, 0, tiled=True)

    first = jnp.arange(held)[:, None, None]
    came = [
        jnp.where(first == way, jnp.broadcast_to(came[way], (held, rows, cols)).astype(F32), 0)
        for way in range(2)
    ]
    for step in range(far - 1, 0, -1):
        added = [base(step, *moving), base(-step, *moving)]
        moving = [(came[way].astype(F32) + added[way]).astype(BF16) for way in range(2)]
        if step == far - 2:
            wanted = pick(key, tie(spread, *moving).reshape(mp * slots, 2, piece, cols))
            wanted = wanted.reshape(mp, held, 2, piece, cols)
            roots = lax.all_to_all(wanted, "mp", 0, 0, tiled=True)
        came = [hop(moving[way], way) for way in range(2)]
    blocks = (
        came[0].astype(F32) + came[1].astype(F32) + base(0, *moving, roots)
    ).astype(BF16)

    result, sliced = precondition(blocks, roots)

    arrived = lax.all_to_all(sliced, "mp", 0, 0, tiled=True)

    shape = (zs, 2, held, rows, cols)
    where = jnp.stack([z, core])
    pieces = []
    flow = [result, result]
    for step in range(1, far):
        flow = [hop(flow[way], way) for way in range(2)]
        if step == far - 2:
            flow = tie(flow, to_owner)
        if step == far - 1:
            flow = tie(flow, own)
        if step == far - 3:
            to_owner = pick(source, tie(arrived, *flow).reshape(mp * held, piece, cols))
            own = lax.all_to_all(
                to_owner.reshape(mp, slots, piece, cols), "mp", 0, 0, tiled=True
            )
        steps = [-step, step]
        if step == far - 1:
            *halves, group = part(*flow)
        elif step == 1:
            steps = [0, *steps]
            group = jnp.stack([result, *flow])
        else:
            group = jnp.stack(flow)
        for cross, value in ((False, group), (True, swap(group))):
            pieces.append(([(at, cross, None) for at in steps], value))
    flow = [hop(halves[way], way) for way in range(2)]
    left_updated, right_updated = statistics(own, left_stats[0, 0], right_stats[0, 0])
    direction = place(tie(where, left_updated), pieces, None, shape)
    pair = jnp.stack(tie(flow, direction))
    late = [
        ([(-far, cross, 0), (far, cross, 1)], value)
        for cross, value in ((False, pair), (True, swap(pair)))
    ]
    direction = place(where, late, direction, shape)
    return (
        direction.reshape(per_shard, rows, cols),
        left_updated[None, None],
        right_updated[None, None],
    )


def solution(mesh):
    split = Mesh(mesh.devices.reshape(-1, 2, mesh.shape["mp"]), ("z", "core", "mp"))
    held = P(DP, "mp", None, None, None)
    in_specs = (P(DP, "mp", None, None), held, held, held, held, P())
    out_specs = (P("mp", None, None), held, held)
    return jax.shard_map(
        per_device, mesh=split, in_specs=in_specs, out_specs=out_specs, check_vma=False
    )
```

```python
import jax
import jax.numpy as jnp
from jax import lax
from jax.experimental import pallas as pl
from jax.experimental.pallas import tpu as pltpu
from jax.sharding import Mesh
from jax.sharding import PartitionSpec as P

DP = ("z", "core")
F32 = jnp.float32
BF16 = jnp.bfloat16
SMEM = pl.BlockSpec(memory_space=pltpu.SMEM)
VMEM = pl.BlockSpec(memory_space=pltpu.VMEM)
ANYWHERE = pl.BlockSpec(memory_space=pl.ANY)
LIMIT = pltpu.CompilerParams(vmem_limit_bytes=12 * 2**20)


def near(value):
    return pltpu.with_memory_space_constraint(value, pltpu.VMEM)


def tie(value, *others):
    return lax.optimization_barrier((value, others))[0]


def pick_kernel(source_ref, value_ref, out_ref):
    def one(i, carry):
        source = source_ref[i]
        piece = value_ref[jnp.maximum(source, 0)]
        out_ref[i] = jnp.where(source >= 0, piece, jnp.zeros_like(piece))
        return carry

    lax.fori_loop(0, out_ref.shape[0], one, 0, unroll=8)


def pick(source, values):
    return pl.pallas_call(
        pick_kernel,
        out_shape=jax.ShapeDtypeStruct((*source.shape, *values.shape[1:]), values.dtype),
        in_specs=[SMEM, VMEM],
        out_specs=VMEM,
        compiler_params=LIMIT,
        name="pick",
    )(source, near(values))


def precond_kernel(grad_ref, root_ref, out_ref, sliced_ref):
    held, rows, cols = grad_ref.shape
    for j in range(held):
        left = root_ref[:, j, 0].reshape(rows, rows)
        right = root_ref[:, j, 1].reshape(cols, cols)
        half = jnp.dot(left, grad_ref[j], preferred_element_type=F32).astype(BF16)
        out_ref[j] = jnp.dot(half, right, preferred_element_type=F32).astype(BF16)
        sliced_ref[:, j] = grad_ref[j].reshape(sliced_ref.shape[0], *sliced_ref.shape[2:])


def precondition(grads, roots):
    held, rows, cols = grads.shape
    peers = roots.shape[0]
    return pl.pallas_call(
        precond_kernel,
        out_shape=(
            jax.ShapeDtypeStruct(grads.shape, BF16),
            jax.ShapeDtypeStruct((peers, held, rows // peers, cols), BF16),
        ),
        in_specs=[VMEM, VMEM],
        out_specs=(VMEM, VMEM),
        compiler_params=LIMIT,
        name="precondition",
    )(near(grads), near(roots))


def part_kernel(up_ref, down_ref, up_part_ref, down_part_ref, pair_ref):
    up_part_ref[...] = up_ref[0:1]
    down_part_ref[...] = down_ref[1:2]
    pair_ref[0] = up_ref[...]
    pair_ref[1] = down_ref[...]


def part(up, down):
    one = jax.ShapeDtypeStruct((1, *up.shape[1:]), BF16)
    return pl.pallas_call(
        part_kernel,
        out_shape=(one, one, jax.ShapeDtypeStruct((2, *up.shape), BF16)),
        in_specs=[VMEM, VMEM],
        out_specs=(VMEM, VMEM, VMEM),
        compiler_params=LIMIT,
        name="part",
    )(near(up), near(down))


def statistics_kernel(own_ref, left_ref, right_ref, left_out_ref, right_out_ref):
    peers, _, piece, cols = own_ref.shape
    own = own_ref[:, pl.program_id(0)].reshape(peers * piece, cols)
    left_out_ref[0] = left_ref[0] + lax.dot_general(
        own, own, (((1,), (1,)), ((), ())), preferred_element_type=F32
    )
    right_out_ref[0] = right_ref[0] + lax.dot_general(
        own, own, (((0,), (0,)), ((), ())), preferred_element_type=F32
    )


def statistics(own, left, right):
    slots = own.shape[1]
    one = pl.BlockSpec((1, *left.shape[1:]), lambda s: (s, 0, 0))
    return pl.pallas_call(
        statistics_kernel,
        grid=(slots,),
        out_shape=(
            jax.ShapeDtypeStruct(left.shape, F32),
            jax.ShapeDtypeStruct(right.shape, F32),
        ),
        in_specs=[VMEM, one, one],
        out_specs=(one, one),
        compiler_params=LIMIT,
        name="statistics",
    )(near(own), *(pltpu.with_memory_space_constraint(x, pltpu.HBM) for x in (left, right)))


def place(where, pieces, direction, shape):
    zs = shape[0]
    fresh = direction is None

    def kernel(where_ref, *refs):
        refs = list(refs)
        sem = refs.pop()
        out_ref = refs.pop()
        if not fresh:
            refs.pop(0)
        z, core = where_ref[0], where_ref[1]
        copies = []
        for ref, (places, value) in zip(refs, pieces):
            for i, (step, cross, part) in enumerate(places):
                at = lax.rem(z + step + zs, zs)
                side = 1 - core if cross else core
                target = out_ref.at[at, side]
                if part is not None:
                    target = target.at[pl.ds(part, 1)]
                copies.append(pltpu.make_async_copy(ref.at[i], target, sem.at[len(copies)]))
        for copy in copies:
            copy.start()
        for copy in copies:
            copy.wait()

    operands = ([] if fresh else [direction]) + [near(value) for _, value in pieces]
    return pl.pallas_call(
        kernel,
        out_shape=jax.ShapeDtypeStruct(shape, BF16),
        in_specs=[SMEM] + ([] if fresh else [ANYWHERE]) + [VMEM] * len(pieces),
        out_specs=ANYWHERE,
        scratch_shapes=[pltpu.SemaphoreType.DMA((sum(len(p) for p, _ in pieces),))],
        input_output_aliases={} if fresh else {1: 0},
        compiler_params=LIMIT,
        name="place",
    )(where, *operands)


def per_device(grad_parts, left_stats, right_stats, left_root, right_root, owners):
    zs = lax.axis_size("z")
    mp = lax.axis_size("mp")
    z = lax.axis_index("z")
    core = lax.axis_index("core")
    dp = z * 2 + core
    _, per_shard, rows, cols = grad_parts.shape
    held = per_shard // (2 * zs)
    slots = left_stats.shape[2]
    piece = rows // mp
    far = zs // 2
    grads = grad_parts.reshape(zs, 2, held, rows, cols)
    ways = [[(i, (i + 1) % zs) for i in range(zs)], [(i, (i - 1) % zs) for i in range(zs)]]

    def hop(value, way):
        return lax.ppermute(value, "z", ways[way])

    def swap(value):
        return lax.ppermute(value, "core", [(0, 1), (1, 0)])

    row_owner = lax.dynamic_slice(
        owners.reshape(mp, 2 * zs, held), (0, dp, 0), (mp, 1, held)
    ).reshape(mp * held)
    pos = jnp.arange(mp * held, dtype=jnp.int32)
    same = (row_owner[:, None] == row_owner[None, :]) & (pos[None, :] < pos[:, None])
    key = row_owner * slots + jnp.sum(same.astype(jnp.int32), axis=1)
    keys = jnp.arange(mp * slots, dtype=jnp.int32)
    hit = keys[:, None] == key[None, :]
    source = jnp.sum(jnp.where(hit, pos[None, :] + 1, 0), axis=1) - 1

    def rows_of(step, which):
        at = (z + step + zs) % zs
        return lax.dynamic_slice(
            grads, (at, which, 0, 0, 0), (1, 1, held, rows, cols)
        ).reshape(held, rows, cols)

    def base(step, *others):
        at = (z + step + zs) % zs
        at = tie(at, *others) if others else at
        given = lax.dynamic_slice(theirs, (at, 0, 0, 0), (1, held, rows, cols))[0]
        mine = lax.dynamic_slice(grads, (at, core, 0, 0, 0), (1, 1, held, rows, cols))
        value = mine.reshape(held, rows, cols).astype(F32) + given.astype(F32)
        return lax.optimization_barrier(value)

    farthest = swap(rows_of(far, 1 - core))
    theirs = lax.dynamic_slice(
        grads, (0, 1 - core, 0, 0, 0), (zs, 1, held, rows, cols)
    ).reshape(zs, held, rows, cols)
    moving = lax.optimization_barrier(rows_of(far, core))
    moving = [
        (moving[way : way + 1].astype(F32) + farthest[way : way + 1].astype(F32)).astype(BF16)
        for way in range(2)
    ]
    theirs = swap(tie(theirs, *moving))
    came = [hop(moving[way], way) for way in range(2)]

    spread = jnp.stack([left_root[0, 0], right_root[0, 0]], axis=1).reshape(
        slots, 2, mp, piece, cols
    )
    spread = jnp.moveaxis(tie(spread, *moving), 2, 0)
    spread = lax.all_to_all(spread, "mp", 0, 0, tiled=True)

    first = jnp.arange(held)[:, None, None]
    came = [
        jnp.where(first == way, jnp.broadcast_to(came[way], (held, rows, cols)).astype(F32), 0)
        for way in range(2)
    ]
    for step in range(far - 1, 0, -1):
        added = [base(step, *moving), base(-step, *moving)]
        moving = [(came[way].astype(F32) + added[way]).astype(BF16) for way in range(2)]
        if step == far - 2:
            wanted = pick(key, tie(spread, *moving).reshape(mp * slots, 2, piece, cols))
            wanted = wanted.reshape(mp, held, 2, piece, cols)
            roots = lax.all_to_all(wanted, "mp", 0, 0, tiled=True)
        came = [hop(moving[way], way) for way in range(2)]
    blocks = (
        came[0].astype(F32) + came[1].astype(F32) + base(0, *moving, roots)
    ).astype(BF16)

    result, sliced = precondition(blocks, roots)

    arrived = lax.all_to_all(sliced, "mp", 0, 0, tiled=True)

    shape = (zs, 2, held, rows, cols)
    where = jnp.stack([z, core])
    pieces = []
    flow = [result, result]
    for step in range(1, far):
        flow = [hop(flow[way], way) for way in range(2)]
        if step == far - 2:
            flow = tie(flow, to_owner)
        if step == far - 1:
            flow = tie(flow, own)
        if step == far - 3:
            to_owner = pick(source, tie(arrived, *flow).reshape(mp * held, piece, cols))
            own = lax.all_to_all(
                to_owner.reshape(mp, slots, piece, cols), "mp", 0, 0, tiled=True
            )
        steps = [-step, step]
        if step == far - 1:
            *halves, group = part(*flow)
        elif step == 1:
            steps = [0, *steps]
            group = jnp.stack([result, *flow])
        else:
            group = jnp.stack(flow)
        for cross, value in ((False, group), (True, swap(group))):
            pieces.append(([(at, cross, None) for at in steps], value))
    flow = [hop(halves[way], way) for way in range(2)]
    left_updated, right_updated = statistics(own, left_stats[0, 0], right_stats[0, 0])
    direction = place(tie(where, left_updated), pieces, None, shape)
    pair = jnp.stack(tie(flow, direction))
    late = [
        ([(-far, cross, 0), (far, cross, 1)], value)
        for cross, value in ((False, pair), (True, swap(pair)))
    ]
    direction = place(where, late, direction, shape)
    return (
        direction.reshape(per_shard, rows, cols),
        left_updated[None, None],
        right_updated[None, None],
    )


def solution(mesh):
    split = Mesh(mesh.devices.reshape(-1, 2, mesh.shape["mp"]), ("z", "core", "mp"))
    held = P(DP, "mp", None, None, None)
    in_specs = (P(DP, "mp", None, None), held, held, held, held, P())
    out_specs = (P("mp", None, None), held, held)
    return jax.shard_map(
        per_device, mesh=split, in_specs=in_specs, out_specs=out_specs, check_vma=False
    )
```

```python
import jax
import jax.numpy as jnp
from jax import lax
from jax.experimental import pallas as pl
from jax.experimental.pallas import tpu as pltpu
from jax.sharding import Mesh
from jax.sharding import PartitionSpec as P

DP = ("z", "core")
F32 = jnp.float32
BF16 = jnp.bfloat16
SMEM = pl.BlockSpec(memory_space=pltpu.SMEM)
VMEM = pl.BlockSpec(memory_space=pltpu.VMEM)
ANYWHERE = pl.BlockSpec(memory_space=pl.ANY)
LIMIT = pltpu.CompilerParams(vmem_limit_bytes=12 * 2**20)


def near(value):
    return pltpu.with_memory_space_constraint(value, pltpu.VMEM)


def tie(value, *others):
    return lax.optimization_barrier((value, others))[0]


def pick_kernel(source_ref, value_ref, out_ref):
    def one(i, carry):
        source = source_ref[i]
        piece = value_ref[jnp.maximum(source, 0)]
        out_ref[i] = jnp.where(source >= 0, piece, jnp.zeros_like(piece))
        return carry

    lax.fori_loop(0, out_ref.shape[0], one, 0, unroll=8)


def pick(source, values):
    return pl.pallas_call(
        pick_kernel,
        out_shape=jax.ShapeDtypeStruct((*source.shape, *values.shape[1:]), values.dtype),
        in_specs=[SMEM, VMEM],
        out_specs=VMEM,
        compiler_params=LIMIT,
        name="pick",
    )(source, near(values))


def precond_kernel(grad_ref, root_ref, out_ref, sliced_ref):
    held, rows, cols = grad_ref.shape
    for j in range(held):
        left = root_ref[:, j, 0].reshape(rows, rows)
        right = root_ref[:, j, 1].reshape(cols, cols)
        half = jnp.dot(left, grad_ref[j], preferred_element_type=F32).astype(BF16)
        out_ref[j] = jnp.dot(half, right, preferred_element_type=F32).astype(BF16)
        sliced_ref[:, j] = grad_ref[j].reshape(sliced_ref.shape[0], *sliced_ref.shape[2:])


def precondition(grads, roots):
    held, rows, cols = grads.shape
    peers = roots.shape[0]
    return pl.pallas_call(
        precond_kernel,
        out_shape=(
            jax.ShapeDtypeStruct(grads.shape, BF16),
            jax.ShapeDtypeStruct((peers, held, rows // peers, cols), BF16),
        ),
        in_specs=[VMEM, VMEM],
        out_specs=(VMEM, VMEM),
        compiler_params=LIMIT,
        name="precondition",
    )(near(grads), near(roots))


def part_kernel(up_ref, down_ref, up_part_ref, down_part_ref, pair_ref):
    up_part_ref[...] = up_ref[0:1]
    down_part_ref[...] = down_ref[1:2]
    pair_ref[0] = up_ref[...]
    pair_ref[1] = down_ref[...]


def part(up, down):
    one = jax.ShapeDtypeStruct((1, *up.shape[1:]), BF16)
    return pl.pallas_call(
        part_kernel,
        out_shape=(one, one, jax.ShapeDtypeStruct((2, *up.shape), BF16)),
        in_specs=[VMEM, VMEM],
        out_specs=(VMEM, VMEM, VMEM),
        compiler_params=LIMIT,
        name="part",
    )(near(up), near(down))


def statistics_kernel(own_ref, left_ref, right_ref, left_out_ref, right_out_ref):
    peers, _, piece, cols = own_ref.shape
    own = own_ref[:, pl.program_id(0)].reshape(peers * piece, cols)
    left_out_ref[0] = left_ref[0] + lax.dot_general(
        own, own, (((1,), (1,)), ((), ())), preferred_element_type=F32
    )
    right_out_ref[0] = right_ref[0] + lax.dot_general(
        own, own, (((0,), (0,)), ((), ())), preferred_element_type=F32
    )


def statistics(own, left, right):
    slots = own.shape[1]
    one = pl.BlockSpec((1, *left.shape[1:]), lambda s: (s, 0, 0))
    return pl.pallas_call(
        statistics_kernel,
        grid=(slots,),
        out_shape=(
            jax.ShapeDtypeStruct(left.shape, F32),
            jax.ShapeDtypeStruct(right.shape, F32),
        ),
        in_specs=[VMEM, one, one],
        out_specs=(one, one),
        compiler_params=LIMIT,
        name="statistics",
    )(near(own), *(pltpu.with_memory_space_constraint(x, pltpu.HBM) for x in (left, right)))


def place(where, pieces, direction, shape):
    zs = shape[0]
    fresh = direction is None

    def kernel(where_ref, *refs):
        refs = list(refs)
        sem = refs.pop()
        out_ref = refs.pop()
        if not fresh:
            refs.pop(0)
        z, core = where_ref[0], where_ref[1]
        copies = []
        for ref, (places, value) in zip(refs, pieces):
            for i, (step, cross, part) in enumerate(places):
                at = lax.rem(z + step + zs, zs)
                side = 1 - core if cross else core
                target = out_ref.at[at, side]
                if part is not None:
                    target = target.at[pl.ds(part, 1)]
                copies.append(pltpu.make_async_copy(ref.at[i], target, sem.at[len(copies)]))
        for copy in copies:
            copy.start()
        for copy in copies:
            copy.wait()

    operands = ([] if fresh else [direction]) + [near(value) for _, value in pieces]
    return pl.pallas_call(
        kernel,
        out_shape=jax.ShapeDtypeStruct(shape, BF16),
        in_specs=[SMEM] + ([] if fresh else [ANYWHERE]) + [VMEM] * len(pieces),
        out_specs=ANYWHERE,
        scratch_shapes=[pltpu.SemaphoreType.DMA((sum(len(p) for p, _ in pieces),))],
        input_output_aliases={} if fresh else {1: 0},
        compiler_params=LIMIT,
        name="place",
    )(where, *operands)


def per_device(grad_parts, left_stats, right_stats, left_root, right_root, owners):
    zs = lax.axis_size("z")
    mp = lax.axis_size("mp")
    z = lax.axis_index("z")
    core = lax.axis_index("core")
    dp = z * 2 + core
    _, per_shard, rows, cols = grad_parts.shape
    held = per_shard // (2 * zs)
    slots = left_stats.shape[2]
    piece = rows // mp
    far = zs // 2
    grads = grad_parts.reshape(zs, 2, held, rows, cols)
    ways = [[(i, (i + 1) % zs) for i in range(zs)], [(i, (i - 1) % zs) for i in range(zs)]]

    def hop(value, way):
        return lax.ppermute(value, "z", ways[way])

    def swap(value):
        return lax.ppermute(value, "core", [(0, 1), (1, 0)])

    row_owner = lax.dynamic_slice(
        owners.reshape(mp, 2 * zs, held), (0, dp, 0), (mp, 1, held)
    ).reshape(mp * held)
    pos = jnp.arange(mp * held, dtype=jnp.int32)
    same = (row_owner[:, None] == row_owner[None, :]) & (pos[None, :] < pos[:, None])
    key = row_owner * slots + jnp.sum(same.astype(jnp.int32), axis=1)
    keys = jnp.arange(mp * slots, dtype=jnp.int32)
    hit = keys[:, None] == key[None, :]
    source = jnp.sum(jnp.where(hit, pos[None, :] + 1, 0), axis=1) - 1

    def rows_of(step, which):
        at = (z + step + zs) % zs
        return lax.dynamic_slice(
            grads, (at, which, 0, 0, 0), (1, 1, held, rows, cols)
        ).reshape(held, rows, cols)

    def base(step, *others):
        at = (z + step + zs) % zs
        at = tie(at, *others) if others else at
        given = lax.dynamic_slice(theirs, (at, 0, 0, 0), (1, held, rows, cols))[0]
        mine = lax.dynamic_slice(grads, (at, core, 0, 0, 0), (1, 1, held, rows, cols))
        value = mine.reshape(held, rows, cols).astype(F32) + given.astype(F32)
        return lax.optimization_barrier(value)

    farthest = swap(rows_of(far, 1 - core))
    theirs = lax.dynamic_slice(
        grads, (0, 1 - core, 0, 0, 0), (zs, 1, held, rows, cols)
    ).reshape(zs, held, rows, cols)
    moving = lax.optimization_barrier(rows_of(far, core))
    moving = [
        (moving[way : way + 1].astype(F32) + farthest[way : way + 1].astype(F32)).astype(BF16)
        for way in range(2)
    ]
    theirs = swap(tie(theirs, *moving))
    came = [hop(moving[way], way) for way in range(2)]

    both = tie((left_root[0, 0], right_root[0, 0]), *moving)
    spread = jnp.stack(both, axis=1).reshape(slots, 2, mp, piece, cols)
    spread = jnp.moveaxis(spread, 2, 0)
    spread = lax.all_to_all(spread, "mp", 0, 0, tiled=True)

    first = jnp.arange(held)[:, None, None]
    came = [
        jnp.where(first == way, jnp.broadcast_to(came[way], (held, rows, cols)).astype(F32), 0)
        for way in range(2)
    ]
    for step in range(far - 1, 0, -1):
        added = [base(step, *moving), base(-step, *moving)]
        moving = [(came[way].astype(F32) + added[way]).astype(BF16) for way in range(2)]
        if step == far - 2:
            wanted = pick(key, tie(spread, *moving).reshape(mp * slots, 2, piece, cols))
            wanted = wanted.reshape(mp, held, 2, piece, cols)
            roots = lax.all_to_all(wanted, "mp", 0, 0, tiled=True)
        came = [hop(moving[way], way) for way in range(2)]
    blocks = (
        came[0].astype(F32) + came[1].astype(F32) + base(0, *moving, roots)
    ).astype(BF16)

    result, sliced = precondition(blocks, roots)

    arrived = lax.all_to_all(sliced, "mp", 0, 0, tiled=True)

    shape = (zs, 2, held, rows, cols)
    where = jnp.stack([z, core])
    pieces = []
    flow = [result, result]
    for step in range(1, far):
        flow = [hop(flow[way], way) for way in range(2)]
        if step == far - 2:
            flow = tie(flow, to_owner)
        if step == far - 1:
            flow = tie(flow, own)
        if step == far - 3:
            to_owner = pick(source, tie(arrived, *flow).reshape(mp * held, piece, cols))
            own = lax.all_to_all(
                to_owner.reshape(mp, slots, piece, cols), "mp", 0, 0, tiled=True
            )
        steps = [-step, step]
        if step == far - 1:
            *halves, group = part(*flow)
        elif step == 1:
            steps = [0, *steps]
            group = jnp.stack([result, *flow])
        else:
            group = jnp.stack(flow)
        for cross, value in ((False, group), (True, swap(group))):
            pieces.append(([(at, cross, None) for at in steps], value))
    flow = [hop(halves[way], way) for way in range(2)]
    left_updated, right_updated = statistics(own, left_stats[0, 0], right_stats[0, 0])
    direction = place(tie(where, left_updated), pieces, None, shape)
    pair = jnp.stack(tie(flow, direction))
    late = [
        ([(-far, cross, 0), (far, cross, 1)], value)
        for cross, value in ((False, pair), (True, swap(pair)))
    ]
    direction = place(where, late, direction, shape)
    return (
        direction.reshape(per_shard, rows, cols),
        left_updated[None, None],
        right_updated[None, None],
    )


def solution(mesh):
    split = Mesh(mesh.devices.reshape(-1, 2, mesh.shape["mp"]), ("z", "core", "mp"))
    held = P(DP, "mp", None, None, None)
    in_specs = (P(DP, "mp", None, None), held, held, held, held, P())
    out_specs = (P("mp", None, None), held, held)
    return jax.shard_map(
        per_device, mesh=split, in_specs=in_specs, out_specs=out_specs, check_vma=False
    )
```
